32 devices in a mesh: bank: 2 (over x), tmpl: 16 (over z, y, core).
Axes of the slice: x: 2, y: 2, z: 4, core: 2. Of those that a mesh axis runs over, the one named last changes fastest.
Arguments:
- strain_fast: bfloat16 [9216], replicated, may hold values from -6 to 6
- strain_half: bfloat16 [8704], replicated, may hold values from -6 to 6
- strain_quarter: bfloat16 [8448], replicated, may hold values from -6 to 6
- strain_eighth: bfloat16 [8320], replicated, may hold values from -6 to 6
- basis_taps: bfloat16 [8, 512, 8192], P('bank', 'tmpl'), parts along dimension 0, may hold values from -0.0625 to 0.0625
- recon_coeffs: bfloat16 [8, 4096, 512], P('bank', 'tmpl'), parts along dimension 0, may hold values from -0.25 to 0.25
Outputs:
- snr_series: bfloat16 [8192, 1024], P(('bank', 'tmpl')), parts along dimension 0
- peak_snr: float32 [2048], P('bank'), parts along dimension 0
The draws below stay inside these ranges and needn't reach their ends.
There are 2 independent parts, one for each index of `bank`. The reference program is written for one: setup_inputs(seed, part) draws one part's arguments, and reference() takes and returns one part's arrays. A program takes and returns all parts, laid end to end along the dimension named above; an argument that names none is the same for every part. Nothing has to cross between parts.
All inputs are finite; a program needn't handle non-finite values.
Results may differ from the reference program's by a relative error of at most 0.0049.
Values may be sent and summed in bfloat16 or wider, within the bound.
A program may use at most 128 MiB of HBM per device.

```python
import jax
import jax.numpy as jnp
from jax import lax

BASES = 512
TAPS = 8192
TEMPLATES = 4096
SAMPLES = 1024


def block_levels(rng, shape, pieces, low, high):
    def one(position, blocks):
        draws = jax.random.uniform(jax.random.fold_in(jax.random.fold_in(rng, 6), position), (blocks,), jnp.float32, low / len(pieces), high / len(pieces))
        return jnp.repeat(jnp.exp(draws), shape[position] // blocks).reshape((-1,) + (1,) * (len(shape) - position - 1))

    factor_of = one(*pieces[0])
    for cut in pieces[1:]:
        factor_of = factor_of * one(*cut)
    return factor_of


def gaussian(key, dims, scale, reach, pieces=(), dtype=jnp.bfloat16):
    gain = block_levels(key, dims, pieces, -0.22, 0.18) if pieces else 1.0
    array = jax.random.normal(key, dims, jnp.float32) * scale * gain
    return jnp.minimum(jnp.maximum(array, -reach), reach).astype(dtype)


def setup_inputs(seed: int = 0, part: int = 0) -> dict:
    seeds = jax.random.split(jax.random.key(seed), 7)
    part_keys = jax.random.split(jax.random.fold_in(seeds[6], part), 7)
    strain_fast = gaussian(seeds[0], (SAMPLES + TAPS,), 1.0, 6.0)
    strain_half = gaussian(seeds[1], (SAMPLES // 2 + TAPS,), 1.0, 6.0)
    strain_quarter = gaussian(seeds[2], (SAMPLES // 4 + TAPS,), 1.0, 6.0)
    strain_eighth = gaussian(seeds[3], (SAMPLES // 8 + TAPS,), 1.0, 6.0)
    basis_taps = gaussian(part_keys[4], (4, BASES, TAPS), TAPS ** -0.5, 0.0625, ((1, 16),))
    recon_coeffs = gaussian(part_keys[5], (4, TEMPLATES, BASES), BASES ** -0.5, 0.25, ((1, 16),))
    return dict(strain_fast=strain_fast, strain_half=strain_half, strain_quarter=strain_quarter, strain_eighth=strain_eighth, basis_taps=basis_taps, recon_coeffs=recon_coeffs)


def correlate(strain, taps):
    signal = strain.astype(jnp.float32)[None, None, :]
    kernel = taps.astype(jnp.float32)[:, None, :]
    filtered = lax.conv_general_dilated(signal, kernel, (1,), "VALID", dimension_numbers=("NCH", "OIH", "NCH"), precision=lax.Precision.HIGHEST)
    sample_count = strain.shape[0] - taps.shape[1]
    return filtered[0, :, :sample_count].astype(jnp.bfloat16)


def reference(strain_fast, strain_half, strain_quarter, strain_eighth, basis_taps, recon_coeffs):
    streams = (strain_fast, strain_half, strain_quarter, strain_eighth)
    running = None
    for section in (3, 2, 1, 0):
        basis_out = correlate(streams[section], basis_taps[section])
        summed = jnp.dot(recon_coeffs[section], basis_out, preferred_element_type=jnp.float32)
        if section == 3:
            running = summed
        else:
            running = summed + jnp.repeat(running, 2, axis=1)
    return running.astype(jnp.bfloat16), jnp.max(jnp.abs(running), axis=0)
```

```python
import functools

import jax
import jax.numpy as jnp
from jax import lax
from jax.experimental import pallas as pl
from jax.experimental.pallas import tpu as pltpu
from jax.sharding import PartitionSpec as P

LANES = 128
BLOCK = 256
UNROLL = 9
PARTS = 3


def shifted_rows(rows_ref, filled, tiles):
    width = tiles * LANES
    zero = jnp.zeros((8, LANES), jnp.float32)
    rows = jnp.concatenate(
        [jnp.broadcast_to(rows_ref[m : m + 1, :], (8, LANES)) if m < filled else zero for m in range(tiles)], axis=1
    )
    index = lax.broadcasted_iota(jnp.int32, (8, width), 0)
    for bit in range(3):
        moved = pltpu.roll(rows, width - (1 << bit), 1)
        rows = jnp.where((index >> bit) & 1 == 1, moved, rows)
    return rows


def doubled(values):
    rows = values.shape[0]
    lane = lax.broadcasted_iota(jnp.int32, (rows, LANES), 1)
    pieces = []
    for tile in range(values.shape[1] // LANES):
        source = values[:, tile * LANES : (tile + 1) * LANES]
        for half in range(2):
            index = lane // 2 + half * (LANES // 2)
            pieces.append(jnp.take_along_axis(source, index, axis=1, mode="promise_in_bounds"))
    return jnp.concatenate(pieces, axis=1)


def kernel(n, counts, *refs):
    sections = len(counts)
    x_hbm = refs[:sections]
    taps_hbm, coef_hbm, snr_ref, peak_ref = refs[sections : sections + 4]
    gathered = refs[sections + 4 : 2 * sections + 4]
    x_refs = refs[2 * sections + 4 : 3 * sections + 4]
    scratch = refs[3 * sections + 4 :]
    wide, shifted, taps_ref, coef_ref, total_ref, series, peaks = scratch[:7]
    local_sem, along_sem, across_sem, mate_sem, recv_sem, pair_sem, peak_sem = scratch[7:]
    rows, tap_count = taps_hbm.shape[1], taps_hbm.shape[2]
    lead = taps_ref.shape[2] - tap_count - tail_of(counts, tap_count)
    lines = n // 4
    me = lax.axis_index("tmpl")
    core = lax.rem(me, 2)
    side = lax.rem(me // 2, 2)
    spot = me // 4

    def device(at, y, c):
        return at * 4 + y * 2 + c

    across, mate = device(spot, 1 - side, core), device(spot, side, 1 - core)

    barrier = pltpu.get_barrier_semaphore()
    for step in range(1, n):
        pl.semaphore_signal(barrier, inc=1, device_id={"tmpl": lax.rem(me + step, n)}, device_id_type=pl.DeviceIdType.MESH)

    taps_in = [
        pltpu.make_async_copy(taps_hbm.at[s], taps_ref.at[s, :, pl.ds(lead, tap_count)], local_sem.at[s])
        for s in range(sections)
    ]
    coef_in = pltpu.make_async_copy(coef_hbm, coef_ref, local_sem.at[sections])
    x_in = [pltpu.make_async_copy(x_hbm[s], x_refs[s], local_sem.at[sections + 1 + s]) for s in range(sections)]
    for s in range(sections):
        x_in[s].start()
        taps_in[s].start()
    coef_in.start()
    for s in range(sections):
        taps_ref[s, :, :lead] = jnp.zeros((rows, lead), jnp.bfloat16)
        after = taps_ref.shape[2] - lead - tap_count
        taps_ref[s, :, lead + tap_count :] = jnp.zeros((rows, after), jnp.bfloat16)

    def convolve(s):
        width = min(BLOCK, counts[s])
        groups = counts[s] // width
        filled = x_refs[s].shape[0]
        x_in[s].wait()
        wide[:filled, :] = x_refs[s][...].astype(jnp.float32)
        shifted[...] = shifted_rows(wide, filled, shifted.shape[1] // LANES)
        taps_in[s].wait()
        steps = -(-(groups - 1 + tap_count // BLOCK) // UNROLL)
        window = (2 * UNROLL + 2) * LANES

        def body(step, total):
            start = pl.multiple_of(step * (UNROLL * BLOCK), BLOCK)
            base = shifted[:, pl.ds(start, window)]
            grown = [base] + [pltpu.roll(base, window - 8 * g, 1) for g in range(1, LANES // 8)]
            frames = jnp.concatenate(grown, axis=0).astype(jnp.bfloat16)
            weights = jnp.concatenate([frames[:, at : at + width] for at in range(0, UNROLL * BLOCK, LANES)], axis=0)
            left = jnp.concatenate(
                [
                    taps_ref[s, :, pl.ds(pl.multiple_of(start + (lead - a * BLOCK), BLOCK), UNROLL * BLOCK)]
                    for a in range(groups)
                ],
                axis=0,
            )
            return total + jnp.dot(left, weights, preferred_element_type=jnp.float32)

        total = jnp.zeros((groups * rows, width), jnp.float32)
        cuts = [steps * part // PARTS for part in range(PARTS + 1)]
        for part in range(PARTS):
            total = lax.fori_loop(cuts[part], cuts[part + 1], body, total)
        out = total.astype(jnp.bfloat16)
        for a in range(groups):
            gathered[s][me, :, a * width : (a + 1) * width] = out[a * rows : (a + 1) * rows]

    def remote(s, part, send_sem, recv_sem, to):
        return pltpu.make_async_remote_copy(
            src_ref=gathered[s].at[part],
            dst_ref=gathered[s].at[part],
            send_sem=send_sem.at[s],
            recv_sem=recv_sem,
            device_id={"tmpl": to},
            device_id_type=pl.DeviceIdType.MESH,
        )

    def to_line(s, slot, to):
        return remote(s, slot, along_sem, recv_sem.at[s, slot // 2], to)

    def to_across(s, slot):
        return remote(s, slot, across_sem, recv_sem.at[s, slot // 2], across)

    def to_mate(s, part):
        return remote(s, part, mate_sem, pair_sem.at[s], mate)

    def both_ways(k, handle):
        for way in (1, -1):
            origin = spot - way * k
            pl.when((origin >= 0) & (origin < lines))(functools.partial(handle, origin, spot + way))

    def own(s):
        to_across(s, me).start()
        for way in (1, -1):
            to = spot + way
            pl.when((to >= 0) & (to < lines))(lambda to=to: to_line(s, me, device(to, side, core)).start())
        to_mate(s, me).start()

    def along(s, k):
        def handle(origin, onward):
            slot = device(origin, side, core)
            to_across(s, slot).wait_recv()
            pl.when((onward >= 0) & (onward < lines))(lambda: to_line(s, slot, device(onward, side, core)).start())
            to_across(s, slot).start()
            to_mate(s, slot).start()

        both_ways(k, handle)

    def beside(s, k):
        def handle(origin, onward):
            slot = device(origin, 1 - side, core)
            to_across(s, slot).wait_recv()
            to_mate(s, slot).start()

        handle(spot, None) if k == 0 else both_ways(k, handle)

    def some(count):
        return pl.ds(0, count)

    def sent(s):
        to_mate(s, some(2 * lines)).wait_send()
        remote(s, some(lines), across_sem, pair_sem.at[s], across).wait_send()
        for at in range(lines):
            count = (at + 1 if at < lines - 1 else 0) + (lines - at if at > 0 else 0)
            if count:
                pl.when(spot == at)(lambda count=count: remote(s, some(count), along_sem, pair_sem.at[s], mate).wait_send())

    def combine(s):
        basis = gathered[s][...].reshape(n * rows, counts[s])
        return jnp.dot(coef_ref[s], basis, preferred_element_type=jnp.float32)

    running = {}
    for s in range(sections):
        convolve(s)
        if s == 0:
            pl.semaphore_wait(barrier, n - 1)
        own(s)
    coef_in.wait()
    for k in range(1, lines):
        for s in range(sections):
            along(s, k)
        for s in range(sections):
            beside(s, k - 1)
    for s in range(sections):
        beside(s, lines - 1)
    for s in range(sections):
        to_mate(s, some(2 * lines)).wait_recv()
        if s == 0:
            total_ref[...] = combine(0)
        else:
            running[s] = combine(s)

    upper = running[sections - 1]
    for s in reversed(range(1, sections - 1)):
        upper = running[s] + doubled(upper)
    total = total_ref[...] + doubled(upper)
    peaks[me] = jnp.max(jnp.abs(total), axis=0, keepdims=True)

    def peak_copy(part, to):
        return pltpu.make_async_remote_copy(
            src_ref=peaks.at[part],
            dst_ref=peaks.at[part],
            send_sem=peak_sem.at[0],
            recv_sem=peak_sem.at[1],
            device_id={"tmpl": to},
            device_id_type=pl.DeviceIdType.MESH,
        )

    others = [lax.rem(me + step, n) for step in range(1, n)]
    for other in others:
        peak_copy(me, other).start()
    series[...] = total.astype(jnp.bfloat16)
    series_out = pltpu.make_async_copy(series, snr_ref, local_sem.at[3 * sections])
    series_out.start()
    for s in range(sections):
        sent(s)
    peak_copy(some(n - 1), mate).wait_recv()
    peak_copy(some(n - 1), mate).wait_send()
    peak_ref[...] = jnp.max(peaks[...], axis=0)
    series_out.wait()


def tail_of(counts, tap_count):
    groups = max(counts) // BLOCK
    steps = -(-(groups - 1 + tap_count // BLOCK) // UNROLL)
    return steps * UNROLL * BLOCK - tap_count


def fused(n, streams, basis_taps, recon_coeffs):
    sections, rows, tap_count = basis_taps.shape
    templates, bases = recon_coeffs.shape[1:]
    counts = tuple(stream.shape[0] - tap_count for stream in streams)
    tail = tail_of(counts, tap_count)
    width = tap_count + tail + 2 * LANES
    lead = (max(counts) // BLOCK - 1) * BLOCK
    tiles = [stream.reshape(-1, LANES) for stream in streams]
    snr, peak = pl.pallas_call(
        functools.partial(kernel, n, counts),
        out_shape=(
            jax.ShapeDtypeStruct((templates, counts[0]), jnp.bfloat16),
            jax.ShapeDtypeStruct((1, counts[0]), jnp.float32),
        ),
        in_specs=[pl.BlockSpec(memory_space=pltpu.HBM)] * (sections + 2),
        out_specs=(pl.BlockSpec(memory_space=pltpu.HBM), pl.BlockSpec(memory_space=pltpu.VMEM)),
        scratch_shapes=[pltpu.VMEM((n, rows, count), jnp.bfloat16) for count in counts]
        + [pltpu.VMEM(tile.shape, jnp.bfloat16) for tile in tiles]
        + [
            pltpu.VMEM((max(tile.shape[0] for tile in tiles), LANES), jnp.float32),
            pltpu.VMEM((8, width), jnp.float32),
            pltpu.VMEM((sections, rows, lead + tap_count + tail), jnp.bfloat16),
            pltpu.VMEM((sections, templates, bases), jnp.bfloat16),
            pltpu.VMEM((templates, counts[0]), jnp.float32),
            pltpu.VMEM((templates, counts[0]), jnp.bfloat16),
            pltpu.VMEM((n, 1, counts[0]), jnp.float32),
            pltpu.SemaphoreType.DMA((3 * sections + 1,)),
            pltpu.SemaphoreType.DMA((sections,)),
            pltpu.SemaphoreType.DMA((sections,)),
            pltpu.SemaphoreType.DMA((sections,)),
            pltpu.SemaphoreType.DMA((sections, n // 2)),
            pltpu.SemaphoreType.DMA((sections,)),
            pltpu.SemaphoreType.DMA((2,)),
        ],
        compiler_params=pltpu.CompilerParams(collective_id=0, has_side_effects=True, vmem_limit_bytes=63500000),
    )(*tiles, basis_taps, recon_coeffs)
    return snr, peak.reshape(counts[0])


def correlate(strain, bases_dev):
    tap_count = bases_dev.shape[1]
    sample_count = strain.shape[0] - tap_count
    stride = min(256, sample_count)
    extent = stride + tap_count

    def frame_block(number):
        segment = lax.dynamic_slice_in_dim(strain, number * stride, extent)
        repeated = jnp.tile(segment, stride + 1)[: stride * (extent + 1)]
        frames = repeated.reshape(stride, extent + 1)[:, :tap_count]
        product = lax.dot_general(bases_dev, frames, (((1,), (1,)), ((), ())), preferred_element_type=jnp.float32)
        return product.astype(jnp.bfloat16)

    pieces = lax.map(frame_block, jnp.arange(sample_count // stride, dtype=jnp.int32))
    return jnp.transpose(pieces, (1, 0, 2)).reshape(bases_dev.shape[0], sample_count)


def general(streams, basis_taps, recon_coeffs):
    counts = [stream.shape[0] - basis_taps.shape[2] for stream in streams]
    joined = jnp.concatenate([correlate(stream, taps) for stream, taps in zip(streams, basis_taps)], axis=1)
    basis = lax.all_gather(joined, "tmpl", axis=0, tiled=True)
    running, end = None, basis.shape[1]
    for section in reversed(range(len(counts))):
        columns = basis[:, end - counts[section] : end]
        end -= counts[section]
        summed = jnp.dot(recon_coeffs[section], columns, preferred_element_type=jnp.float32)
        running = summed if running is None else summed + jnp.repeat(running, 2, axis=1)
    return running.astype(jnp.bfloat16), lax.pmax(jnp.max(jnp.abs(running), axis=0), "tmpl")


def suits(n, streams, basis_taps, recon_coeffs):
    tap_count = basis_taps.shape[2]
    counts = [stream.shape[0] - tap_count for stream in streams]
    return (
        n % 4 == 0
        and basis_taps.shape[1] % 16 == 0
        and recon_coeffs.shape[1] % 16 == 0
        and tap_count % BLOCK == 0
        and counts[0] % BLOCK == 0
        and all(c % BLOCK == 0 or c == LANES for c in counts)
        and all(a == 2 * b for a, b in zip(counts, counts[1:]))
    )


def solution(mesh):
    n = mesh.shape["tmpl"]

    def per_device(strain_fast, strain_half, strain_quarter, strain_eighth, basis_taps, recon_coeffs):
        streams = (strain_fast, strain_half, strain_quarter, strain_eighth)
        if suits(n, streams, basis_taps, recon_coeffs):
            return fused(n, streams, basis_taps, recon_coeffs)
        return general(streams, basis_taps, recon_coeffs)

    in_specs = (P(), P(), P(), P(), P("bank", "tmpl", None), P("bank", "tmpl", None))
    out_specs = (P(("bank", "tmpl"), None), P("bank"))
    return jax.shard_map(per_device, mesh=mesh, in_specs=in_specs, out_specs=out_specs, check_vma=False)
```

```python
import functools

import jax
import jax.numpy as jnp
from jax import lax
from jax.experimental import pallas as pl
from jax.experimental.pallas import tpu as pltpu
from jax.sharding import PartitionSpec as P

LANES = 128
BLOCK = 256
UNROLL = 9
PARTS = 3


def shifted_rows(rows_ref, filled, tiles):
    width = tiles * LANES
    zero = jnp.zeros((8, LANES), jnp.float32)
    rows = jnp.concatenate(
        [jnp.broadcast_to(rows_ref[m : m + 1, :], (8, LANES)) if m < filled else zero for m in range(tiles)], axis=1
    )
    index = lax.broadcasted_iota(jnp.int32, (8, width), 0)
    for bit in range(3):
        moved = pltpu.roll(rows, width - (1 << bit), 1)
        rows = jnp.where((index >> bit) & 1 == 1, moved, rows)
    return rows


def doubled(values):
    rows = values.shape[0]
    lane = lax.broadcasted_iota(jnp.int32, (rows, LANES), 1)
    pieces = []
    for tile in range(values.shape[1] // LANES):
        source = values[:, tile * LANES : (tile + 1) * LANES]
        for half in range(2):
            index = lane // 2 + half * (LANES // 2)
            pieces.append(jnp.take_along_axis(source, index, axis=1, mode="promise_in_bounds"))
    return jnp.concatenate(pieces, axis=1)


def kernel(n, counts, *refs):
    sections = len(counts)
    x_hbm = refs[:sections]
    taps_hbm, coef_hbm, snr_ref, peak_ref = refs[sections : sections + 4]
    gathered = refs[sections + 4 : 2 * sections + 4]
    x_refs = refs[2 * sections + 4 : 3 * sections + 4]
    scratch = refs[3 * sections + 4 :]
    wide, shifted, taps_ref, coef_ref, total_ref, peaks = scratch[:6]
    local_sem, along_sem, across_sem, mate_sem, recv_sem, pair_sem, peak_sem = scratch[6:]
    rows, tap_count = taps_hbm.shape[1], taps_hbm.shape[2]
    lead = taps_ref.shape[2] - tap_count - tail_of(counts, tap_count)
    lines = n // 4
    me = lax.axis_index("tmpl")
    core = lax.rem(me, 2)
    side = lax.rem(me // 2, 2)
    spot = me // 4

    def device(at, y, c):
        return at * 4 + y * 2 + c

    across, mate = device(spot, 1 - side, core), device(spot, side, 1 - core)

    barrier = pltpu.get_barrier_semaphore()

    def greet(to):
        pl.semaphore_signal(barrier, inc=1, device_id={"tmpl": to}, device_id_type=pl.DeviceIdType.MESH)

    greet(mate)
    greet(across)
    pl.when(spot + 1 < lines)(lambda: greet(device(spot + 1, side, core)))
    pl.when(spot - 1 >= 0)(lambda: greet(device(spot - 1, side, core)))
    greeted = 2 + (spot + 1 < lines).astype(jnp.int32) + (spot - 1 >= 0).astype(jnp.int32)

    taps_in = [
        pltpu.make_async_copy(taps_hbm.at[s], taps_ref.at[s, :, pl.ds(lead, tap_count)], local_sem.at[s])
        for s in range(sections)
    ]
    coef_in = pltpu.make_async_copy(coef_hbm, coef_ref, local_sem.at[sections])
    x_in = [pltpu.make_async_copy(x_hbm[s], x_refs[s], local_sem.at[sections + 1 + s]) for s in range(sections)]
    for s in range(sections):
        x_in[s].start()
        taps_in[s].start()
    coef_in.start()
    for s in range(sections):
        taps_ref[s, :, :lead] = jnp.zeros((rows, lead), jnp.bfloat16)
        after = taps_ref.shape[2] - lead - tap_count
        taps_ref[s, :, lead + tap_count :] = jnp.zeros((rows, after), jnp.bfloat16)

    def convolve(s, serve):
        width = min(BLOCK, counts[s])
        groups = counts[s] // width
        filled = x_refs[s].shape[0]
        x_in[s].wait()
        wide[:filled, :] = x_refs[s][...].astype(jnp.float32)
        shifted[...] = shifted_rows(wide, filled, shifted.shape[1] // LANES)
        taps_in[s].wait()
        steps = -(-(groups - 1 + tap_count // BLOCK) // UNROLL)
        window = (2 * UNROLL + 2) * LANES

        def body(step, total):
            start = pl.multiple_of(step * (UNROLL * BLOCK), BLOCK)
            base = shifted[:, pl.ds(start, window)]
            grown = [base] + [pltpu.roll(base, window - 8 * g, 1) for g in range(1, LANES // 8)]
            frames = jnp.concatenate(grown, axis=0).astype(jnp.bfloat16)
            weights = jnp.concatenate([frames[:, at : at + width] for at in range(0, UNROLL * BLOCK, LANES)], axis=0)
            left = jnp.concatenate(
                [
                    taps_ref[s, :, pl.ds(pl.multiple_of(start + (lead - a * BLOCK), BLOCK), UNROLL * BLOCK)]
                    for a in range(groups)
                ],
                axis=0,
            )
            return total + jnp.dot(left, weights, preferred_element_type=jnp.float32)

        total = jnp.zeros((groups * rows, width), jnp.float32)
        cuts = [steps * part // PARTS for part in range(PARTS + 1)]
        for part in range(PARTS):
            total = lax.fori_loop(cuts[part], cuts[part + 1], body, total)
            if part < PARTS - 1:
                serve((s, part))
        out = total.astype(jnp.bfloat16)
        for a in range(groups):
            gathered[s][me, :, a * width : (a + 1) * width] = out[a * rows : (a + 1) * rows]

    chunks = chunks_of(counts, rows)

    def remote(c, slot, send_sem, recv_sem, to):
        s, first, height = chunks[c]
        part = gathered[s].at[slot, pl.ds(first, height)]
        return pltpu.make_async_remote_copy(
            src_ref=part,
            dst_ref=part,
            send_sem=send_sem.at[c],
            recv_sem=recv_sem,
            device_id={"tmpl": to},
            device_id_type=pl.DeviceIdType.MESH,
        )

    def to_line(c, slot, to):
        return remote(c, slot, along_sem, recv_sem.at[c, slot // 2], to)

    def to_across(c, slot):
        return remote(c, slot, across_sem, recv_sem.at[c, slot // 2], across)

    def to_mate(c, slot):
        return remote(c, slot, mate_sem, pair_sem.at[c], mate)

    def both_ways(k, handle):
        for way in (1, -1):
            origin = spot - way * k
            pl.when((origin >= 0) & (origin < lines))(functools.partial(handle, origin, spot + way))

    def own(c):
        to_across(c, me).start()
        for way in (1, -1):
            to = spot + way
            pl.when((to >= 0) & (to < lines))(lambda to=to: to_line(c, me, device(to, side, core)).start())
        to_mate(c, me).start()

    def along(c, k):
        def handle(origin, onward):
            slot = device(origin, side, core)
            to_across(c, slot).wait_recv()
            to_across(c, slot).start()
            pl.when((onward >= 0) & (onward < lines))(lambda: to_line(c, slot, device(onward, side, core)).start())
            to_mate(c, slot).start()

        both_ways(k, handle)

    def beside(c, k):
        def handle(origin, onward):
            slot = device(origin, 1 - side, core)
            to_across(c, slot).wait_recv()
            to_mate(c, slot).start()

        handle(spot, None) if k == 0 else both_ways(k, handle)

    def some(count):
        return pl.ds(0, count)

    def sent(c):
        to_mate(c, some(2 * lines)).wait_send()
        remote(c, some(lines), across_sem, pair_sem.at[c], across).wait_send()
        for at in range(lines):
            count = (at + 1 if at < lines - 1 else 0) + (lines - at if at > 0 else 0)
            if count:
                pl.when(spot == at)(lambda count=count: remote(c, some(count), along_sem, pair_sem.at[c], mate).wait_send())

    def combine(s):
        basis = gathered[s][...].reshape(n * rows, counts[s])
        return jnp.dot(coef_ref[s], basis, preferred_element_type=jnp.float32)

    pieces = range(len(chunks))
    early = {}
    order = []
    for k in range(1, lines):
        order += [(along, c, k) for c in pieces] + [(beside, c, k - 1) for c in pieces]
    order += [(beside, c, lines - 1) for c in pieces]
    done = set()

    def serve(at):
        for event in early.get(at, []):
            event[0](*event[1:])
            done.add(event)

    running = {}
    for s in range(sections):
        convolve(s, serve)
        if s == 0:
            pl.semaphore_wait(barrier, greeted)
        for c, chunk in enumerate(chunks):
            if chunk[0] == s:
                own(c)
        serve((s, PARTS - 1))
    coef_in.wait()
    for event in order:
        if event not in done:
            event[0](*event[1:])
    for c, chunk in enumerate(chunks):
        to_mate(c, some(2 * lines)).wait_recv()
        if chunk[0] == 0 and chunk[1] > 0 or chunk[2] == rows and chunk[0] == 0:
            total_ref[...] = combine(0)
        elif chunk[0] > 0:
            running[chunk[0]] = combine(chunk[0])

    upper = running[sections - 1]
    for s in reversed(range(1, sections - 1)):
        upper = running[s] + doubled(upper)
    total = total_ref[...] + doubled(upper)
    peaks[me] = jnp.max(jnp.abs(total), axis=0, keepdims=True)

    def peak_copy(part, to):
        return pltpu.make_async_remote_copy(
            src_ref=peaks.at[part],
            dst_ref=peaks.at[part],
            send_sem=peak_sem.at[0],
            recv_sem=peak_sem.at[1],
            device_id={"tmpl": to},
            device_id_type=pl.DeviceIdType.MESH,
        )

    others = [lax.rem(me + step, n) for step in range(1, n)]
    for other in others:
        peak_copy(me, other).start()
    snr_ref[...] = total.astype(jnp.bfloat16)
    for c in range(len(chunks)):
        sent(c)
    peak_copy(some(n - 1), mate).wait_recv()
    peak_copy(some(n - 1), mate).wait_send()
    peak_ref[...] = jnp.max(peaks[...], axis=0)


def chunks_of(counts, rows):
    halves = 2 if rows % 32 == 0 else 1
    height = rows // halves
    return [(0, height * half, height) for half in range(halves)] + [(s, 0, rows) for s in range(1, len(counts))]


def tail_of(counts, tap_count):
    groups = max(counts) // BLOCK
    steps = -(-(groups - 1 + tap_count // BLOCK) // UNROLL)
    return steps * UNROLL * BLOCK - tap_count


def fused(n, streams, basis_taps, recon_coeffs):
    sections, rows, tap_count = basis_taps.shape
    templates, bases = recon_coeffs.shape[1:]
    counts = tuple(stream.shape[0] - tap_count for stream in streams)
    tail = tail_of(counts, tap_count)
    width = tap_count + tail + 2 * LANES
    lead = (max(counts) // BLOCK - 1) * BLOCK
    pieces = len(chunks_of(counts, rows))
    tiles = [stream.reshape(-1, LANES) for stream in streams]
    snr, peak = pl.pallas_call(
        functools.partial(kernel, n, counts),
        out_shape=(
            jax.ShapeDtypeStruct((templates, counts[0]), jnp.bfloat16),
            jax.ShapeDtypeStruct((1, counts[0]), jnp.float32),
        ),
        in_specs=[pl.BlockSpec(memory_space=pltpu.HBM)] * (sections + 2),
        out_specs=(pl.BlockSpec(memory_space=pltpu.VMEM), pl.BlockSpec(memory_space=pltpu.VMEM)),
        scratch_shapes=[pltpu.VMEM((n, rows, count), jnp.bfloat16) for count in counts]
        + [pltpu.VMEM(tile.shape, jnp.bfloat16) for tile in tiles]
        + [
            pltpu.VMEM((max(tile.shape[0] for tile in tiles), LANES), jnp.float32),
            pltpu.VMEM((8, width), jnp.float32),
            pltpu.VMEM((sections, rows, lead + tap_count + tail), jnp.bfloat16),
            pltpu.VMEM((sections, templates, bases), jnp.bfloat16),
            pltpu.VMEM((templates, counts[0]), jnp.float32),
            pltpu.VMEM((n, 1, counts[0]), jnp.float32),
            pltpu.SemaphoreType.DMA((2 * sections + 1,)),
            pltpu.SemaphoreType.DMA((pieces,)),
            pltpu.SemaphoreType.DMA((pieces,)),
            pltpu.SemaphoreType.DMA((pieces,)),
            pltpu.SemaphoreType.DMA((pieces, n // 2)),
            pltpu.SemaphoreType.DMA((pieces,)),
            pltpu.SemaphoreType.DMA((2,)),
        ],
        compiler_params=pltpu.CompilerParams(collective_id=0, has_side_effects=True, vmem_limit_bytes=40000000),
    )(*[pltpu.with_memory_space_constraint(array, pltpu.HBM) for array in (*tiles, basis_taps, recon_coeffs)])
    return snr, peak.reshape(counts[0])


def correlate(strain, bases_dev):
    tap_count = bases_dev.shape[1]
    sample_count = strain.shape[0] - tap_count
    stride = min(256, sample_count)
    extent = stride + tap_count

    def frame_block(number):
        segment = lax.dynamic_slice_in_dim(strain, number * stride, extent)
        repeated = jnp.tile(segment, stride + 1)[: stride * (extent + 1)]
        frames = repeated.reshape(stride, extent + 1)[:, :tap_count]
        product = lax.dot_general(bases_dev, frames, (((1,), (1,)), ((), ())), preferred_element_type=jnp.float32)
        return product.astype(jnp.bfloat16)

    pieces = lax.map(frame_block, jnp.arange(sample_count // stride, dtype=jnp.int32))
    return jnp.transpose(pieces, (1, 0, 2)).reshape(bases_dev.shape[0], sample_count)


def general(streams, basis_taps, recon_coeffs):
    counts = [stream.shape[0] - basis_taps.shape[2] for stream in streams]
    joined = jnp.concatenate([correlate(stream, taps) for stream, taps in zip(streams, basis_taps)], axis=1)
    basis = lax.all_gather(joined, "tmpl", axis=0, tiled=True)
    running, end = None, basis.shape[1]
    for section in reversed(range(len(counts))):
        columns = basis[:, end - counts[section] : end]
        end -= counts[section]
        summed = jnp.dot(recon_coeffs[section], columns, preferred_element_type=jnp.float32)
        running = summed if running is None else summed + jnp.repeat(running, 2, axis=1)
    return running.astype(jnp.bfloat16), lax.pmax(jnp.max(jnp.abs(running), axis=0), "tmpl")


def suits(n, streams, basis_taps, recon_coeffs):
    tap_count = basis_taps.shape[2]
    counts = [stream.shape[0] - tap_count for stream in streams]
    return (
        n % 4 == 0
        and basis_taps.shape[1] % 16 == 0
        and recon_coeffs.shape[1] % 16 == 0
        and tap_count % BLOCK == 0
        and counts[0] % BLOCK == 0
        and all(c % BLOCK == 0 or c == LANES for c in counts)
        and all(a == 2 * b for a, b in zip(counts, counts[1:]))
    )


def solution(mesh):
    n = mesh.shape["tmpl"]

    def per_device(strain_fast, strain_half, strain_quarter, strain_eighth, basis_taps, recon_coeffs):
        streams = (strain_fast, strain_half, strain_quarter, strain_eighth)
        if suits(n, streams, basis_taps, recon_coeffs):
            return fused(n, streams, basis_taps, recon_coeffs)
        return general(streams, basis_taps, recon_coeffs)

    in_specs = (P(), P(), P(), P(), P("bank", "tmpl", None), P("bank", "tmpl", None))
    out_specs = (P(("bank", "tmpl"), None), P("bank"))
    return jax.shard_map(per_device, mesh=mesh, in_specs=in_specs, out_specs=out_specs, check_vma=False)
```

```python
import functools

import jax
import jax.numpy as jnp
from jax import lax
from jax.experimental import pallas as pl
from jax.experimental.pallas import tpu as pltpu
from jax.sharding import PartitionSpec as P

LANES = 128
BLOCK = 256
UNROLL = 18
CUTS = 1, 1
DEPTH = 16


def shifted_rows(rows_ref, filled, tiles):
    width = tiles * LANES
    zero = jnp.zeros((8, LANES), jnp.float32)
    rows = jnp.concatenate(
        [jnp.broadcast_to(rows_ref[m : m + 1, :], (8, LANES)) if m < filled else zero for m in range(tiles)], axis=1
    )
    index = lax.broadcasted_iota(jnp.int32, (8, width), 0)
    for bit in range(3):
        moved = pltpu.roll(rows, width - (1 << bit), 1)
        rows = jnp.where((index >> bit) & 1 == 1, moved, rows)
    return jnp.concatenate([rows, pltpu.roll(rows, width - 8, 1)], axis=0).astype(jnp.bfloat16)


def doubled(values):
    rows = values.shape[0]
    lane = lax.broadcasted_iota(jnp.int32, (rows, LANES), 1)
    pieces = []
    for tile in range(values.shape[1] // LANES):
        source = values[:, tile * LANES : (tile + 1) * LANES]
        for half in range(2):
            index = lane // 2 + half * (LANES // 2)
            pieces.append(jnp.take_along_axis(source, index, axis=1, mode="promise_in_bounds"))
    return jnp.concatenate(pieces, axis=1)


def kernel(n, counts, *refs):
    sections = len(counts)
    x_hbm = refs[:sections]
    taps_hbm, coef_hbm, snr_ref, peak_ref = refs[sections : sections + 4]
    blocks = groups_of(counts)
    gathered = refs[sections + 4 : sections + 4 + len(blocks)]
    x_refs = refs[sections + 4 + len(blocks) : 2 * sections + 4 + len(blocks)]
    scratch = refs[2 * sections + 4 + len(blocks) :]
    places = {}
    for b, block in enumerate(blocks):
        for s in block:
            places[s] = b, sum(counts[block[0] : s])
    wide, shifted, taps_ref, coef_ref, total_ref, peaks = scratch[:6]
    local_sem, along_sem, across_sem, mate_sem, recv_sem, pair_sem, peak_sem = scratch[6:]
    rows, tap_count = taps_hbm.shape[1], taps_hbm.shape[2]
    lead = taps_ref.shape[2] - tap_count - tail_of(counts, tap_count)
    lines = n // 4
    me = lax.axis_index("tmpl")
    core = lax.rem(me, 2)
    side = lax.rem(me // 2, 2)
    spot = me // 4

    def device(at, y, c):
        return at * 4 + y * 2 + c

    across, mate = device(spot, 1 - side, core), device(spot, side, 1 - core)

    barrier = pltpu.get_barrier_semaphore()

    def greet(to):
        pl.semaphore_signal(barrier, inc=1, device_id={"tmpl": to}, device_id_type=pl.DeviceIdType.MESH)

    greet(mate)
    greet(across)
    pl.when(spot + 1 < lines)(lambda: greet(device(spot + 1, side, core)))
    pl.when(spot - 1 >= 0)(lambda: greet(device(spot - 1, side, core)))
    greeted = 2 + (spot + 1 < lines).astype(jnp.int32) + (spot - 1 >= 0).astype(jnp.int32)

    taps_in = [
        pltpu.make_async_copy(taps_hbm.at[s], taps_ref.at[s, :, pl.ds(lead, tap_count)], local_sem.at[s])
        for s in range(sections)
    ]
    coef_in = pltpu.make_async_copy(coef_hbm, coef_ref, local_sem.at[sections])
    x_in = [pltpu.make_async_copy(x_hbm[s], x_refs[s], local_sem.at[sections + 1 + s]) for s in range(sections)]
    for s in range(sections):
        x_in[s].start()
        taps_in[s].start()
    coef_in.start()
    for s in range(sections):
        taps_ref[s, :, :lead] = jnp.zeros((rows, lead), jnp.bfloat16)
        after = taps_ref.shape[2] - lead - tap_count
        taps_ref[s, :, lead + tap_count :] = jnp.zeros((rows, after), jnp.bfloat16)

    def prepare(s):
        filled = x_refs[s].shape[0]
        x_in[s].wait()
        wide[:filled, :] = x_refs[s][...].astype(jnp.float32)
        shifted[s] = shifted_rows(wide, filled, shifted.shape[2] // LANES)
        taps_in[s].wait()

    def product(s, step):
        width = min(BLOCK, counts[s])
        window = (2 * UNROLL + 2) * LANES
        start = pl.multiple_of(step * (UNROLL * BLOCK), BLOCK)
        base = shifted[s, :, pl.ds(start, window)]
        grown = [base] + [pltpu.roll(base, window - DEPTH * g, 1) for g in range(1, LANES // DEPTH)]
        frames = jnp.concatenate(grown, axis=0)
        weights = jnp.concatenate([frames[:, at : at + width] for at in range(0, UNROLL * BLOCK, LANES)], axis=0)
        left = jnp.concatenate(
            [
                taps_ref[s, :, pl.ds(pl.multiple_of(start + (lead - a * BLOCK), BLOCK), UNROLL * BLOCK)]
                for a in range(counts[s] // width)
            ],
            axis=0,
        )
        return jnp.dot(left, weights, preferred_element_type=jnp.float32)

    def convolve(group):
        for s in group:
            prepare(s)
        widths = [min(BLOCK, counts[s]) for s in group]
        groups = [counts[s] // width for s, width in zip(group, widths)]
        steps = max(-(-(g - 1 + tap_count // BLOCK) // UNROLL) for g in groups)

        def body(step, totals):
            return tuple(total + product(s, step) for s, total in zip(group, totals))

        zeros = tuple(jnp.zeros((g * rows, width), jnp.float32) for g, width in zip(groups, widths))
        totals = lax.fori_loop(0, steps, body, zeros)
        for s, g, width, total in zip(group, groups, widths, totals):
            out = total.astype(jnp.bfloat16)
            b, at = places[s]
            for a in range(g):
                gathered[b][me, :, at + a * width : at + (a + 1) * width] = out[a * rows : (a + 1) * rows]

    chunks = chunks_of(counts, rows)

    def remote(c, slot, send_sem, recv_sem, to):
        b, first, height = chunks[c]
        part = gathered[b].at[slot, pl.ds(first, height)]
        return pltpu.make_async_remote_copy(
            src_ref=part,
            dst_ref=part,
            send_sem=send_sem.at[c],
            recv_sem=recv_sem,
            device_id={"tmpl": to},
            device_id_type=pl.DeviceIdType.MESH,
        )

    def to_line(c, slot, to):
        return remote(c, slot, along_sem, recv_sem.at[c, slot // 2], to)

    def to_across(c, slot):
        return remote(c, slot, across_sem, recv_sem.at[c, slot // 2], across)

    def to_mate(c, slot):
        return remote(c, slot, mate_sem, pair_sem.at[c], mate)

    def both_ways(k, handle):
        for way in (1, -1):
            origin = spot - way * k
            pl.when((origin >= 0) & (origin < lines))(functools.partial(handle, origin, spot + way))

    def own(c):
        to_across(c, me).start()
        for way in (1, -1):
            to = spot + way
            pl.when((to >= 0) & (to < lines))(lambda to=to: to_line(c, me, device(to, side, core)).start())
        to_mate(c, me).start()

    def along(c, k):
        def handle(origin, onward):
            slot = device(origin, side, core)
            to_across(c, slot).wait_recv()
            to_across(c, slot).start()
            pl.when((onward >= 0) & (onward < lines))(lambda: to_line(c, slot, device(onward, side, core)).start())
            to_mate(c, slot).start()

        both_ways(k, handle)

    def beside(c, k):
        def handle(origin, onward):
            slot = device(origin, 1 - side, core)
            to_across(c, slot).wait_recv()
            to_mate(c, slot).start()

        handle(spot, None) if k == 0 else both_ways(k, handle)

    def some(count):
        return pl.ds(0, count)

    def sent(c):
        to_mate(c, some(2 * lines)).wait_send()
        remote(c, some(lines), across_sem, pair_sem.at[c], across).wait_send()
        for at in range(lines):
            count = (at + 1 if at < lines - 1 else 0) + (lines - at if at > 0 else 0)
            if count:
                pl.when(spot == at)(lambda count=count: remote(c, some(count), along_sem, pair_sem.at[c], mate).wait_send())

    def combine(s):
        b, at = places[s]
        basis = gathered[b][:, :, at : at + counts[s]].reshape(n * rows, counts[s])
        return jnp.dot(coef_ref[s], basis, preferred_element_type=jnp.float32)

    pieces = range(len(chunks))
    order = []
    for k in range(1, lines):
        order += [(along, c, k) for c in pieces] + [(beside, c, k - 1) for c in pieces]
    order += [(beside, c, lines - 1) for c in pieces]

    running = {}
    for b, block in enumerate(blocks):
        convolve(block)
        if b == 0:
            pl.semaphore_wait(barrier, greeted)
        for c in pieces:
            if chunks[c][0] == b:
                own(c)
    coef_in.wait()
    for step, c, k in order:
        step(c, k)
    for b, block in enumerate(blocks):
        for c in pieces:
            if chunks[c][0] == b:
                to_mate(c, some(2 * lines)).wait_recv()
        for s in block:
            if s == 0:
                total_ref[...] = combine(0)
            else:
                running[s] = combine(s)

    upper = running[sections - 1]
    for s in reversed(range(1, sections - 1)):
        upper = running[s] + doubled(upper)
    total = total_ref[...] + doubled(upper)
    peaks[me] = jnp.max(jnp.abs(total), axis=0, keepdims=True)

    def peak_copy(part, to):
        return pltpu.make_async_remote_copy(
            src_ref=peaks.at[part],
            dst_ref=peaks.at[part],
            send_sem=peak_sem.at[0],
            recv_sem=peak_sem.at[1],
            device_id={"tmpl": to},
            device_id_type=pl.DeviceIdType.MESH,
        )

    others = [lax.rem(me + step, n) for step in range(1, n)]
    for other in others:
        peak_copy(me, other).start()
    snr_ref[...] = total.astype(jnp.bfloat16)
    for c in range(len(chunks)):
        sent(c)
    peak_copy(some(n - 1), mate).wait_recv()
    peak_copy(some(n - 1), mate).wait_send()
    peak_ref[...] = jnp.max(peaks[...], axis=0)


def groups_of(counts):
    return (range(1), range(1, len(counts)))


def chunks_of(counts, rows):
    chunks = []
    for b in range(len(groups_of(counts))):
        cuts = CUTS[b] if rows % 32 == 0 else 1
        chunks += [(b, rows // cuts * cut, rows // cuts) for cut in range(cuts)]
    return chunks


def tail_of(counts, tap_count):
    groups = max(counts) // BLOCK
    steps = -(-(groups - 1 + tap_count // BLOCK) // UNROLL)
    return steps * UNROLL * BLOCK - tap_count


def fused(n, streams, basis_taps, recon_coeffs):
    sections, rows, tap_count = basis_taps.shape
    templates, bases = recon_coeffs.shape[1:]
    counts = tuple(stream.shape[0] - tap_count for stream in streams)
    tail = tail_of(counts, tap_count)
    width = tap_count + tail + 2 * LANES
    lead = (max(counts) // BLOCK - 1) * BLOCK
    pieces = len(chunks_of(counts, rows))
    tiles = [stream.reshape(-1, LANES) for stream in streams]
    snr, peak = pl.pallas_call(
        functools.partial(kernel, n, counts),
        out_shape=(
            jax.ShapeDtypeStruct((templates, counts[0]), jnp.bfloat16),
            jax.ShapeDtypeStruct((1, counts[0]), jnp.float32),
        ),
        in_specs=[pl.BlockSpec(memory_space=pltpu.HBM)] * (sections + 2),
        out_specs=(pl.BlockSpec(memory_space=pltpu.VMEM), pl.BlockSpec(memory_space=pltpu.VMEM)),
        scratch_shapes=[pltpu.VMEM((n, rows, sum(counts[s] for s in block)), jnp.bfloat16) for block in groups_of(counts)]
        + [pltpu.VMEM(tile.shape, jnp.bfloat16) for tile in tiles]
        + [
            pltpu.VMEM((max(tile.shape[0] for tile in tiles), LANES), jnp.float32),
            pltpu.VMEM((sections, DEPTH, width), jnp.bfloat16),
            pltpu.VMEM((sections, rows, lead + tap_count + tail), jnp.bfloat16),
            pltpu.VMEM((sections, templates, bases), jnp.bfloat16),
            pltpu.VMEM((templates, counts[0]), jnp.float32),
            pltpu.VMEM((n, 1, counts[0]), jnp.float32),
            pltpu.SemaphoreType.DMA((2 * sections + 1,)),
            pltpu.SemaphoreType.DMA((pieces,)),
            pltpu.SemaphoreType.DMA((pieces,)),
            pltpu.SemaphoreType.DMA((pieces,)),
            pltpu.SemaphoreType.DMA((pieces, n // 2)),
            pltpu.SemaphoreType.DMA((pieces,)),
            pltpu.SemaphoreType.DMA((2,)),
        ],
        compiler_params=pltpu.CompilerParams(collective_id=0, has_side_effects=True, vmem_limit_bytes=40000000),
    )(*[pltpu.with_memory_space_constraint(array, pltpu.HBM) for array in (*tiles, basis_taps, recon_coeffs)])
    return snr, peak.reshape(counts[0])


def correlate(strain, bases_dev):
    tap_count = bases_dev.shape[1]
    sample_count = strain.shape[0] - tap_count
    stride = min(256, sample_count)
    extent = stride + tap_count

    def frame_block(number):
        segment = lax.dynamic_slice_in_dim(strain, number * stride, extent)
        repeated = jnp.tile(segment, stride + 1)[: stride * (extent + 1)]
        frames = repeated.reshape(stride, extent + 1)[:, :tap_count]
        product = lax.dot_general(bases_dev, frames, (((1,), (1,)), ((), ())), preferred_element_type=jnp.float32)
        return product.astype(jnp.bfloat16)

    pieces = lax.map(frame_block, jnp.arange(sample_count // stride, dtype=jnp.int32))
    return jnp.transpose(pieces, (1, 0, 2)).reshape(bases_dev.shape[0], sample_count)


def general(streams, basis_taps, recon_coeffs):
    counts = [stream.shape[0] - basis_taps.shape[2] for stream in streams]
    joined = jnp.concatenate([correlate(stream, taps) for stream, taps in zip(streams, basis_taps)], axis=1)
    basis = lax.all_gather(joined, "tmpl", axis=0, tiled=True)
    running, end = None, basis.shape[1]
    for section in reversed(range(len(counts))):
        columns = basis[:, end - counts[section] : end]
        end -= counts[section]
        summed = jnp.dot(recon_coeffs[section], columns, preferred_element_type=jnp.float32)
        running = summed if running is None else summed + jnp.repeat(running, 2, axis=1)
    return running.astype(jnp.bfloat16), lax.pmax(jnp.max(jnp.abs(running), axis=0), "tmpl")


def suits(n, streams, basis_taps, recon_coeffs):
    tap_count = basis_taps.shape[2]
    counts = [stream.shape[0] - tap_count for stream in streams]
    return (
        n % 4 == 0
        and basis_taps.shape[1] % 16 == 0
        and recon_coeffs.shape[1] % 16 == 0
        and tap_count % BLOCK == 0
        and counts[0] % BLOCK == 0
        and all(c % BLOCK == 0 or c == LANES for c in counts)
        and all(a == 2 * b for a, b in zip(counts, counts[1:]))
    )


def solution(mesh):
    n = mesh.shape["tmpl"]

    def per_device(strain_fast, strain_half, strain_quarter, strain_eighth, basis_taps, recon_coeffs):
        streams = (strain_fast, strain_half, strain_quarter, strain_eighth)
        if suits(n, streams, basis_taps, recon_coeffs):
            return fused(n, streams, basis_taps, recon_coeffs)
        return general(streams, basis_taps, recon_coeffs)

    in_specs = (P(), P(), P(), P(), P("bank", "tmpl", None), P("bank", "tmpl", None))
    out_specs = (P(("bank", "tmpl"), None), P("bank"))
    return jax.shard_map(per_device, mesh=mesh, in_specs=in_specs, out_specs=out_specs, check_vma=False)
```
